1024 devices in a mesh: grp: 4 (over y_hi), fsdp: 64 (over x, z), tp: 4 (over y_lo, core).
Axes of the slice: x: 4, y: 8 (y_hi: 4, y_lo: 2; y = y_hi * 2 + y_lo), z: 16, core: 2. Of those that a mesh axis runs over, the one named last changes fastest.
Arguments:
- image_rows: bfloat16 [98304, 8192], P(('grp', 'fsdp'), 'tp'), may hold values from -6 to 6
- enc_gain: bfloat16 [8192], P('tp'), may hold values from 0.099609375 to 1.8984375
- key_value_w: bfloat16 [8192, 1024], P(('tp', 'fsdp')), may hold values from -0.0625 to 0.0625
- tiles: int32 [384], P('fsdp'), may hold values from 1 to 4
- queries: bfloat16 [65536, 4096], P(('grp', 'fsdp'), 'tp'), may hold values from -6 to 6
Outputs:
- attended: bfloat16 [65536, 4096], P(('grp', 'fsdp'), 'tp')
The draws below stay inside these ranges and needn't reach their ends.
Inputs may be any that keep to these rules, and one draw needn't show every extreme that they name: Each sample has 1 to 4 tiles.
All inputs are finite; a program needn't handle non-finite values.
Results may differ from the reference program's by a relative error of at most 0.0077.
Values may be sent and summed in bfloat16 or wider, within the bound.
A program may use at most 32 MiB of HBM per device.

```python
import jax
import jax.numpy as jnp
from jax import lax

D = 8192
HD = 128
KVH = 4
QH = 32
TILE_TOK = 16
SAMP = 2
TXT_S = 128
CAP = 64
IMG = 128
TXT = 256
N_GRP = 4
N_FSDP = 64


def touch_ends(entries, stream_key, smallest, top_value):
    shape = entries.shape
    index_at = [jax.random.randint(jax.random.fold_in(stream_key, axis), (), 0, shape[axis]) for axis in range(len(shape))]
    entries = entries.at[tuple(index_at)].set(smallest)
    longest = shape.index(max(shape))
    index_at[longest] = (index_at[longest] + 1) % shape[longest]
    return entries.at[tuple(index_at)].set(top_value)


def block_levels(rng, dims, cuts, smallest, top_value):
    def one(axis_at, parts):
        steps = jax.random.uniform(jax.random.fold_in(jax.random.fold_in(rng, 6), axis_at), (parts,), jnp.float32, smallest / len(cuts), top_value / len(cuts))
        return jnp.repeat(jnp.exp(steps), dims[axis_at] // parts).reshape((-1,) + (1,) * (len(dims) - axis_at - 1))

    level = one(*cuts[0])
    for cut in cuts[1:]:
        level = level * one(*cut)
    return level


def gaussian(stream_key, shape, spread, most, split=(), held_as=jnp.bfloat16):
    loudness = block_levels(stream_key, shape, split, -0.22, 0.18) if split else 1.0
    result = jax.random.normal(stream_key, shape, jnp.float32) * spread * loudness
    return jnp.minimum(jnp.maximum(result, -most), most).astype(held_as)


def setup_inputs(seed: int = 0) -> dict:
    key_list = jax.random.split(jax.random.key(seed), 6)
    return {
        "image_rows": gaussian(key_list[0], (N_GRP * N_FSDP * 3 * IMG, D), 1.0, 6.0, ((0, 256), (1, 4))),
        "enc_gain": jnp.clip(1.0 + 0.18 * jax.random.normal(key_list[1], (D,), jnp.float32), 0.099609375, 1.8984375).astype(jnp.bfloat16),
        "key_value_w": gaussian(key_list[2], (D, KVH * 2 * HD), D ** -0.5, 0.0625, ((0, 256),)),
        "tiles": touch_ends(jax.random.randint(key_list[3], (N_FSDP * 3 * SAMP,), 1, 5), jax.random.fold_in(key_list[3], 1), 1, 4).astype(jnp.int32),
        "queries": gaussian(key_list[4], (N_GRP * N_FSDP * TXT, QH * HD), 1.0, 6.0, ((0, 256), (1, 4))),
    }


def reference(image_rows, enc_gain, key_value_w, tiles, queries):
    rows = image_rows[:N_FSDP * 3 * IMG].astype(jnp.float32)
    mean_sq = lax.optimization_barrier(jnp.mean(rows * rows, axis=1, keepdims=True))
    normed = (rows * lax.rsqrt(mean_sq + 1e-05) * enc_gain.astype(jnp.float32)).astype(jnp.bfloat16)
    kv = jnp.dot(normed, key_value_w, preferred_element_type=jnp.float32).astype(jnp.bfloat16)
    kv = kv.reshape(N_FSDP, 3, SAMP, CAP, KVH, 2, HD)
    keys = jnp.swapaxes(kv[..., 0, :], 0, 1)
    values = jnp.swapaxes(kv[..., 1, :], 0, 1)
    query = queries.reshape(N_GRP, N_FSDP, SAMP, TXT_S, KVH, QH // KVH, HD)
    counts = tiles.reshape(N_FSDP, 3, SAMP) * TILE_TOK
    valid = jnp.arange(CAP)[None, None, None, :] < counts[..., None]
    valid = jnp.swapaxes(valid, 0, 1)
    scale = 1.0 / HD ** 0.5

    def one_group(items):
        q_part, k_part, v_part, live = items
        scores = jnp.einsum('fsikgd,fsjkd->fskgij', q_part.astype(jnp.float32), k_part.astype(jnp.float32)) * scale
        scores = jnp.where(live[:, :, None, None, None, :], scores, -1e+30)
        top = lax.optimization_barrier(jnp.max(scores, axis=-1, keepdims=True))
        expo = jnp.exp(scores - top)
        weights = (expo / lax.optimization_barrier(jnp.sum(expo, axis=-1, keepdims=True))).astype(jnp.bfloat16)
        out = jnp.einsum('fskgij,fsjkd->fsikgd', weights.astype(jnp.float32), v_part.astype(jnp.float32))
        return out.astype(jnp.bfloat16)
    outs = lax.map(one_group, (query[1:], keys, values, valid))
    zero_block = jnp.zeros((1,) + outs.shape[1:], jnp.bfloat16)
    full = jnp.concatenate([zero_block, outs], axis=0)
    return full.reshape(N_GRP * N_FSDP * TXT, QH * HD)
```

```python
import jax
import jax.numpy as jnp
from jax import lax
from jax.experimental import pallas as pl
from jax.experimental.pallas import tpu as pltpu
from jax.sharding import PartitionSpec as P

D = 8192
HD = 128
KVH = 4
QH = 32
TILE_TOK = 16
SAMP = 2
TXT_S = 128
CAP = 64
IMG = 128
NX = 4
NZ = 16
HALF = NZ // 2
PIECE = 32
SPLIT = 384
MESH = pl.DeviceIdType.MESH


def project(
    rows_hbm, gain_ref, w_hbm, out_ref,
    rows, normed, wfull, mine, theirs, packed, stat,
    local_sem, stat_send, stat_recv,
    ax_send, ax_recv, az_send, az_recv, bz_send, bz_recv, bx_send, bx_recv, bf_send, bf_recv,
    core_send, core_recv, y_send, y_recv, ready,
):
    g = lax.axis_index("grp")
    f = lax.axis_index("fsdp")
    t = lax.axis_index("tp")
    x, z = f // NZ, f % NZ
    ylo, core = t // 2, t % 2

    def at(x1, z1):
        return (0, x1 * NZ + z1, t)

    def xs(step):
        return (x + step + NX) % NX

    def zs(step):
        return (z + step + NZ) % NZ

    barrier = pltpu.get_barrier_semaphore()

    @pl.when(g == 0)
    def _():
        own_w = pltpu.make_async_copy(w_hbm, wfull.at[x, z], local_sem.at[0])
        own_rows = pltpu.make_async_copy(rows_hbm, rows, local_sem.at[1])
        own_w.start()
        own_rows.start()
        for d in (1, -1):
            pl.semaphore_signal(barrier, inc=1, device_id=at(x, zs(d)), device_id_type=MESH)
        for d in (1, 2, 3):
            pl.semaphore_signal(barrier, inc=1, device_id=at(xs(d), z), device_id_type=MESH)
            pl.semaphore_signal(barrier, inc=1, device_id=(0, f, (t + d) % 4), device_id_type=MESH)
        for gg in (1, 2, 3):
            for yy in (0, 1):
                pl.semaphore_signal(barrier, inc=1, device_id=(gg, f, yy * 2 + core), device_id_type=MESH)
        own_w.wait()
        pl.semaphore_wait(barrier, 8)

        acols, bcols = pl.ds(0, SPLIT), pl.ds(SPLIT, 1024 - SPLIT)
        sends = []

        def push(src, dst, ssem, rsem, dev):
            c = pltpu.make_async_remote_copy(
                src_ref=src, dst_ref=dst, send_sem=ssem, recv_sem=rsem, device_id=dev, device_id_type=MESH
            )
            c.start()
            sends.append(c)
            return c

        def got(dst, rsem):
            pltpu.make_async_copy(dst, dst, rsem).wait()

        def zdir(d):
            return 1 if d == 0 else -1

        def send_a_z(step):
            for d in (0, 1):
                zz = zs(-zdir(d) * step)
                half = pl.ds(2 * d, 2) if step == HALF - 1 else pl.ds(0, NX)
                ref = wfull.at[half, zz, :, acols]
                push(ref, ref, az_send.at[d, step], az_recv.at[d, step], at(x, zs(zdir(d))))

        def got_a_z(step):
            for d in (0, 1):
                zz = zs(-zdir(d) * (step + 1))
                half = pl.ds(2 * d, 2) if step == HALF - 1 else pl.ds(0, NX)
                got(wfull.at[half, zz, :, acols], az_recv.at[d, step])

        def rows_b(d, last):
            return pl.ds(16 * d, 16) if last else pl.ds(0, PIECE)

        def send_b_z(step):
            for d in (0, 1):
                zz = zs(-zdir(d) * step)
                ref = wfull.at[x, zz, rows_b(d, step == HALF - 1), bcols]
                push(ref, ref, bz_send.at[d, step], bz_recv.at[d, step], at(x, zs(zdir(d))))

        def got_b_z(step):
            for d in (0, 1):
                zz = zs(-zdir(d) * (step + 1))
                got(wfull.at[x, zz, rows_b(d, step == HALF - 1), bcols], bz_recv.at[d, step])

        def held(step):
            if step == 0:
                return [(0, z)]
            if step == HALF:
                return [(0, zs(HALF))]
            return [(0, zs(-step)), (1, zs(step))]

        def send_b_x(step):
            for k, zz in held(step):
                for d in (0, 1):
                    ref = wfull.at[x, zz, :, bcols]
                    push(ref, ref, bx_send.at[d, k, step], bx_recv.at[d, k, step], at(xs(zdir(d)), z))

        def relay_b_x(step):
            for k, zz in held(step):
                for d in (0, 1):
                    xx = xs(-zdir(d))
                    got(wfull.at[xx, zz, :, bcols], bx_recv.at[d, k, step])
                    ref = wfull.at[xx, zz, pl.ds(16 * d, 16), bcols]
                    push(ref, ref, bf_send.at[d, k, step], bf_recv.at[d, k, step], at(xs(zdir(d)), z))

        def got_b_f(step):
            for k, zz in held(step):
                for d in (0, 1):
                    got(wfull.at[xs(2), zz, pl.ds(16 * d, 16), bcols], bf_recv.at[d, k, step])

        own_a = wfull.at[x, z, :, acols]
        send_b_z(0)
        for d in (1, 2, 3):
            push(own_a, own_a, ax_send.at[d - 1], ax_recv.at[d - 1], at(xs(d), z))
        send_b_x(0)

        own_rows.wait()
        total = jnp.zeros((3 * IMG, 128), jnp.float32)
        for j in range(NZ):
            part = rows[:, j * 128:(j + 1) * 128].astype(jnp.float32)
            total = total + part * part
        line = jnp.sum(jnp.transpose(total), axis=0, keepdims=True)
        stat[0] = jnp.broadcast_to(line, (8, 3 * IMG))
        for d in (1, 2, 3):
            push(stat.at[0], stat.at[d], stat_send.at[d - 1], stat_recv.at[d - 1], (0, f, (t + d) % 4))
        for d in (1, 2, 3):
            got(wfull.at[xs(-d), z, :, acols], ax_recv.at[d - 1])
        send_a_z(0)

        def normalise():
            for d in (1, 2, 3):
                got(stat.at[d], stat_recv.at[d - 1])
            squares = (stat[0] + stat[1]) + (stat[2] + stat[3])
            inv = lax.rsqrt(squares[0:1] / D + 1e-05)
            column = jnp.transpose(jnp.broadcast_to(inv, (128, 3 * IMG)))
            for j in range(NZ):
                cols = slice(j * 128, (j + 1) * 128)
                normed[:, cols] = (
                    rows[:, cols].astype(jnp.float32) * column * gain_ref[:, cols].astype(jnp.float32)
                ).astype(jnp.bfloat16)

        for step in range(HALF):
            got_b_z(step)
            if step < HALF - 1:
                send_b_z(step + 1)
            send_b_x(step + 1)
            got_a_z(step)
            if step < HALF - 1:
                send_a_z(step + 1)
            relay_b_x(step)
            if step == 1:
                normalise()
        relay_b_x(HALF)
        for step in range(HALF + 1):
            got_b_f(step)

        def head(h):
            cols = pl.ds(pl.multiple_of(h * 256, 256), 256)
            w = wfull[:, :, :, cols].reshape(NX * NZ * PIECE, 256)
            return jnp.dot(normed[...], w, preferred_element_type=jnp.float32)

        sibling = (0, f, ylo * 2 + 1 - core)
        for k in (0, 1):
            mine[k] = head(2 * k + 1 - core)
            push(mine.at[k], theirs.at[k], core_send.at[k], core_recv.at[k], sibling)
        pl.semaphore_wait(ready, 6)
        for k in (0, 1):
            own = head(2 * k + core)
            got(theirs.at[k], core_recv.at[k])
            packed[k] = (own + theirs[k]).astype(jnp.bfloat16)
            for gg in (1, 2, 3):
                push(
                    packed.at[k, pl.ds((gg - 1) * IMG, IMG)], out_ref.at[ylo],
                    y_send.at[gg - 1, k], y_recv.at[ylo], (gg, f, k * 2 + core),
                )
        for c in sends:
            c.wait_send()

    @pl.when(g > 0)
    def _():
        pl.semaphore_wait(barrier, 2)
        for yy in (0, 1):
            pl.semaphore_signal(ready, inc=1, device_id=(0, f, yy * 2 + core), device_id_type=MESH)
        for yy in (0, 1):
            pltpu.make_async_copy(out_ref.at[yy], out_ref.at[yy], y_recv.at[yy]).wait()


def attend(tiles_ref, part_ref, q_ref, o_ref):
    g = lax.axis_index("grp")

    @pl.when(g == 0)
    def _():
        o_ref[...] = jnp.zeros_like(o_ref)

    @pl.when(g > 0)
    def _():
        kv = (part_ref[0].astype(jnp.float32) + part_ref[1].astype(jnp.float32)).astype(jnp.bfloat16)
        slot = lax.broadcasted_iota(jnp.int32, (TXT_S, CAP), 1)
        for s in range(SAMP):
            keys = kv[s * CAP:(s + 1) * CAP, :HD]
            values = kv[s * CAP:(s + 1) * CAP, HD:]
            live = slot < tiles_ref[(g - 1) * SAMP + s] * TILE_TOK
            for h in range(QH // KVH):
                q = q_ref[s * TXT_S:(s + 1) * TXT_S, h * HD:(h + 1) * HD]
                scores = lax.dot_general(
                    q, keys, (((1,), (1,)), ((), ())), preferred_element_type=jnp.float32
                ) * (1.0 / HD**0.5)
                scores = jnp.where(live, scores, -1e30)
                expo = jnp.exp(scores - jnp.max(scores, axis=-1, keepdims=True))
                weights = (expo / jnp.sum(expo, axis=-1, keepdims=True)).astype(jnp.bfloat16)
                o_ref[s * TXT_S:(s + 1) * TXT_S, h * HD:(h + 1) * HD] = jnp.dot(
                    weights, values, preferred_element_type=jnp.float32
                ).astype(jnp.bfloat16)


def shards(image_rows, enc_gain, key_value_w, tiles, queries):
    dma = pltpu.SemaphoreType.DMA
    anywhere = pl.BlockSpec(memory_space=pl.ANY)
    vmem = pl.BlockSpec(memory_space=pltpu.VMEM)
    parts = pl.pallas_call(
        project,
        out_shape=jax.ShapeDtypeStruct((2, IMG, 2 * HD), jnp.bfloat16),
        in_specs=[anywhere, vmem, anywhere],
        out_specs=anywhere,
        scratch_shapes=[
            pltpu.VMEM((3 * IMG, 2048), jnp.bfloat16),
            pltpu.VMEM((3 * IMG, 2048), jnp.bfloat16),
            pltpu.VMEM((NX, NZ, PIECE, 1024), jnp.bfloat16),
            pltpu.VMEM((2, 3 * IMG, 256), jnp.float32),
            pltpu.VMEM((2, 3 * IMG, 256), jnp.float32),
            pltpu.VMEM((2, 3 * IMG, 256), jnp.bfloat16),
            pltpu.VMEM((4, 8, 3 * IMG), jnp.float32),
            dma((2,)),
            dma((3,)),
            dma((3,)),
            dma((3,)),
            dma((3,)),
            dma((2, HALF)),
            dma((2, HALF)),
            dma((2, HALF)),
            dma((2, HALF)),
            dma((2, 2, HALF + 1)),
            dma((2, 2, HALF + 1)),
            dma((2, 2, HALF + 1)),
            dma((2, 2, HALF + 1)),
            dma((2,)),
            dma((2,)),
            dma((3, 2)),
            dma((2,)),
            pltpu.SemaphoreType.REGULAR,
        ],
        compiler_params=pltpu.CompilerParams(
            collective_id=0, has_side_effects=True, vmem_limit_bytes=32 << 20
        ),
        name="project",
    )(image_rows, enc_gain.reshape(1, -1), key_value_w)
    return pl.pallas_call(
        attend,
        out_shape=jax.ShapeDtypeStruct(queries.shape, jnp.bfloat16),
        in_specs=[pl.BlockSpec(memory_space=pltpu.SMEM), vmem, vmem],
        out_specs=vmem,
        compiler_params=pltpu.CompilerParams(vmem_limit_bytes=16 << 20),
        name="attend",
    )(tiles, parts, queries)


def solution(mesh):
    return jax.shard_map(
        shards,
        mesh=mesh,
        in_specs=(
            P(("grp", "fsdp"), "tp"),
            P("tp"),
            P(("tp", "fsdp"), None),
            P("fsdp"),
            P(("grp", "fsdp"), "tp"),
        ),
        out_specs=P(("grp", "fsdp"), "tp"),
        check_vma=False,
    )
```

```python
import jax
import jax.numpy as jnp
from jax import lax
from jax.experimental import pallas as pl
from jax.experimental.pallas import tpu as pltpu
from jax.sharding import PartitionSpec as P

D = 8192
HD = 128
KVH = 4
QH = 32
TILE_TOK = 16
SAMP = 2
TXT_S = 128
CAP = 64
IMG = 128
NX = 4
NZ = 16
FAR = 6
PIECE = 32
PART = 512
SPARE = 2
MESH = pl.DeviceIdType.MESH


def project(
    rows_hbm, gain_hbm, w_hbm, out_ref,
    rows, gain_ref, inbox, normed, wz, mine, theirs, packed, stat, scale, scale_in,
    local_sem, rows_send, rows_recv, stat_send, stat_recv, scale_send, scale_recv,
    far_send, far_recv, near_send, near_recv, core_send, core_recv, part_send, part_recv, ready,
):
    g = lax.axis_index("grp")
    f = lax.axis_index("fsdp")
    t = lax.axis_index("tp")
    x, z = f // NZ, f % NZ
    ylo, core = t // 2, t % 2

    def xs(step):
        return (x + step + NX) % NX

    def zs(step):
        return (z + step + NZ) % NZ

    def chip(gg, x1, z1, t1):
        return (gg, x1 * NZ + z1, t1)

    barrier = pltpu.get_barrier_semaphore()

    def hello(dev):
        pl.semaphore_signal(barrier, inc=1, device_id=dev, device_id_type=MESH)

    def copy(src, dst, ssem, rsem, dev):
        return pltpu.make_async_remote_copy(
            src_ref=src, dst_ref=dst, send_sem=ssem, recv_sem=rsem, device_id=dev, device_id_type=MESH
        )

    def got(dst, rsem):
        pltpu.make_async_copy(dst, dst, rsem).wait()

    def way(d):
        return 1 if d == 0 else -1

    @pl.when(g == SPARE)
    def _():
        pl.semaphore_wait(barrier, 8)

    @pl.when(g != SPARE)
    def _():
        own_w = pltpu.make_async_copy(w_hbm, wz.at[z], local_sem.at[0])
        own_gain = pltpu.make_async_copy(gain_hbm, gain_ref, local_sem.at[1])
        own_rows = pltpu.make_async_copy(rows_hbm, rows, local_sem.at[2])
        own_w.start()
        own_gain.start()
        for d in (1, -1, FAR, -FAR):
            hello(chip(g, x, zs(d), t))

        @pl.when(g == 0)
        def _():
            own_rows.start()
            for d in (1, 2, 3):
                hello((0, f, (t + d) % 4))
                hello(chip(0, xs(d), z, t))
            for gg in (1, 3):
                for xd in range(NX):
                    hello(chip(gg, xs(xd), z, t))
            for xd in range(NX):
                for yy in (0, 1):
                    hello(chip(SPARE, xs(xd), z, yy * 2 + core))

        @pl.when(g > 0)
        def _():
            for xd in range(NX):
                hello(chip(0, xs(xd), z, t))
                hello(chip(g, xs(xd), z, (1 - ylo) * 2 + core))
            for xd in (1, 2, 3):
                hello(chip(g, xs(xd), z, t))
            hello((g, f, ylo * 2 + 1 - core))

        own_w.wait()
        own_gain.wait()

        @pl.when(g == 0)
        def _():
            pl.semaphore_wait(barrier, 18)

        @pl.when(g > 0)
        def _():
            pl.semaphore_wait(barrier, 16)

        sends = []

        def push(*a):
            c = copy(*a)
            c.start()
            sends.append(c)

        def cols(c):
            return pl.ds(c * PART, PART)

        def moved(o, d):
            return o - way(d)

        def cut(o, d):
            return pl.ds(16 * d, 16) if abs(o) == NZ // 2 else pl.ds(0, PIECE)

        def near(o, d, c):
            m = moved(o, d)
            ref = wz.at[zs(o), cut(m, d), cols(c)]
            push(ref, ref, near_send.at[d, c, m % NZ], near_recv.at[d, c, m % NZ], chip(g, x, zs(way(d)), t))

        def got_near(o, d, c):
            got(wz.at[zs(o), cut(o, d), cols(c)], near_recv.at[d, c, o % NZ])

        for c in (0, 1):
            for d in (0, 1):
                ref = wz.at[z, :, cols(c)]
                push(ref, ref, far_send.at[d, c], far_recv.at[d, c], chip(g, x, zs(FAR * way(d)), t))

        def rows_copy(i, gg, block, xd):
            src = rows_hbm.at[pl.ds(block * IMG, IMG), pl.ds(pl.multiple_of(xs(xd) * PART, PART), PART)]
            return copy(src, inbox.at[x], rows_send.at[i, xd], rows_recv.at[x], chip(gg, xs(xd), z, t))

        targets = ((1, 0), (3, 2), (0, 1))

        def own_inbox():
            src = rows_hbm.at[pl.ds(IMG, IMG), pl.ds(pl.multiple_of(x * PART, PART), PART)]
            return pltpu.make_async_copy(src, inbox.at[x], rows_recv.at[x])

        @pl.when(g == 0)
        def _():
            for xd in range(NX):
                for i, (gg, block) in enumerate(targets):
                    if gg == 0 and xd == 0:
                        own_inbox().start()
                    else:
                        rows_copy(i, gg, block, xd).start()

        for c in (0, 1):
            for d in (0, 1):
                near(0, d, c)

        def stat_copy(d):
            return copy(stat.at[0], stat.at[d], stat_send.at[d - 1], stat_recv.at[d - 1], (0, f, (t + d) % 4))

        @pl.when(g == 0)
        def _():
            own_rows.wait()
            total = jnp.zeros((3 * IMG, 128), jnp.float32)
            for j in range(NZ):
                part = rows[:, j * 128:(j + 1) * 128].astype(jnp.float32)
                total = total + part * part
            line = jnp.sum(jnp.transpose(total), axis=0, keepdims=True)
            stat[0] = jnp.broadcast_to(line, (8, 3 * IMG))
            for d in (1, 2, 3):
                stat_copy(d).start()

        for c in (0, 1):
            for d in (0, 1):
                got_near(-way(d), d, c)
                near(-way(d), d, c)

        def scale_copy(i, gg, block, xd):
            return copy(
                scale.at[block], scale_in.at[x], scale_send.at[i, xd], scale_recv.at[x], chip(gg, xs(xd), z, t)
            )

        @pl.when(g == 0)
        def _():
            for d in (1, 2, 3):
                got(stat.at[d], stat_recv.at[d - 1])
            both = (stat[0] + stat[1]) + (stat[2] + stat[3])
            inv = lax.rsqrt(both / D + 1e-05)
            for block in range(3):
                scale[block] = inv[:, block * IMG:(block + 1) * IMG]
            for xd in range(NX):
                for i, (gg, block) in enumerate(targets):
                    if gg == 0 and xd == 0:
                        pltpu.make_async_copy(scale.at[block], scale_in.at[x], scale_recv.at[x]).start()
                    else:
                        scale_copy(i, gg, block, xd).start()

        for c in (0, 1):
            for d in (0, 1):
                got_near(-2 * way(d), d, c)
                near(-2 * way(d), d, c)
        for c in (0, 1):
            for d in (0, 1):
                got(wz.at[zs(-FAR * way(d)), :, cols(c)], far_recv.at[d, c])
            for d in (0, 1):
                near(-FAR * way(d), d, c)
                near(FAR * way(d), d, c)
        for c in (0, 1):
            for d in (0, 1):
                got_near(-7 * way(d), d, c)
                near(-7 * way(d), d, c)
                got_near(5 * way(d), d, c)
                near(5 * way(d), d, c)

        gains = []
        for j in range(PART // 128):
            pick = gain_ref[j * 128:(j + 1) * 128]
            for i in (1, 2, 3):
                pick = jnp.where(x == i, gain_ref[i * PART + j * 128:i * PART + (j + 1) * 128], pick)
            gains.append(pick.astype(jnp.float32).reshape(1, 128))
        for i in range(NX):
            got(inbox.at[i], rows_recv.at[i])
            got(scale_in.at[i], scale_recv.at[i])
            column = jnp.transpose(jnp.broadcast_to(scale_in[i, 0:1], (128, IMG)))
            for j in range(PART // 128):
                lanes = slice(j * 128, (j + 1) * 128)
                normed[i * IMG:(i + 1) * IMG, lanes] = (
                    inbox[i, :, lanes].astype(jnp.float32) * column * gains[j]
                ).astype(jnp.bfloat16)

        for c in (0, 1):
            for d in (0, 1):
                got_near(-3 * way(d), d, c)
                got_near(-8 * way(d), d, c)
                got_near(4 * way(d), d, c)

        def head(h):
            w = wz[:, :, pl.ds(pl.multiple_of(h * 256, 256), 256)].reshape(PART, 256)
            return jnp.dot(normed[...], w, preferred_element_type=jnp.float32)

        def side(j):
            return ylo if j == 0 else 1 - ylo

        order = (1, 0)
        for j in order:
            mine[j] = head(side(j) * 2 + 1 - core)
            push(mine.at[j], theirs.at[j], core_send.at[j], core_recv.at[j], (g, f, ylo * 2 + 1 - core))

        home = jnp.where(g == 0, SPARE, g)
        slot = x * 2 + ylo

        @pl.when(g == 0)
        def _():
            pl.semaphore_wait(ready, 8)

        def own_part():
            return copy(
                packed.at[0, pl.ds(pl.multiple_of(x * IMG, IMG), IMG)], out_ref.at[slot],
                part_send.at[0, 0], part_recv.at[slot], chip(SPARE, x, z, t),
            )

        for j in order:
            own = head(side(j) * 2 + core)
            got(theirs.at[j], core_recv.at[j])
            packed[j] = (own + theirs[j]).astype(jnp.bfloat16)
            for xd in (2, 1, 3, 0):
                src = packed.at[j, pl.ds(pl.multiple_of(xs(xd) * IMG, IMG), IMG)]
                if j == 0 and xd == 0:
                    @pl.when(g == 0)
                    def _():
                        own_part().start()

                    @pl.when(g > 0)
                    def _():
                        pltpu.make_async_copy(src, out_ref.at[slot], part_recv.at[slot]).start()
                else:
                    push(
                        src, out_ref.at[slot], part_send.at[j, xd], part_recv.at[slot],
                        chip(home, xs(xd), z, side(j) * 2 + core),
                    )

        @pl.when(g == 0)
        def _():
            own_part().wait_send()
            for d in (1, 2, 3):
                stat_copy(d).wait_send()
            for xd in range(NX):
                for i, (gg, block) in enumerate(targets):
                    if gg != 0 or xd != 0:
                        rows_copy(i, gg, block, xd).wait_send()
                        scale_copy(i, gg, block, xd).wait_send()

        for c in sends:
            c.wait_send()

    @pl.when(g == SPARE)
    def _():
        for xd in range(NX):
            for yy in (0, 1):
                pl.semaphore_signal(
                    ready, inc=1, device_id=chip(0, xs(xd), z, yy * 2 + core), device_id_type=MESH
                )

    @pl.when(g > 0)
    def _():
        for i in range(2 * NX):
            got(out_ref.at[i], part_recv.at[i])


def attend(tiles_ref, part_ref, q_ref, o_ref):
    g = lax.axis_index("grp")

    @pl.when(g == 0)
    def _():
        o_ref[...] = jnp.zeros_like(o_ref)

    @pl.when(g > 0)
    def _():
        kv = part_ref[0].astype(jnp.float32)
        for i in range(1, 2 * NX):
            kv = kv + part_ref[i].astype(jnp.float32)
        kv = kv.astype(jnp.bfloat16)
        slot = lax.broadcasted_iota(jnp.int32, (TXT_S, CAP), 1)
        for s in range(SAMP):
            keys = kv[s * CAP:(s + 1) * CAP, :HD]
            values = kv[s * CAP:(s + 1) * CAP, HD:]
            live = slot < tiles_ref[(g - 1) * SAMP + s] * TILE_TOK
            for h in range(QH // KVH):
                q = q_ref[s * TXT_S:(s + 1) * TXT_S, h * HD:(h + 1) * HD]
                scores = lax.dot_general(
                    q, keys, (((1,), (1,)), ((), ())), preferred_element_type=jnp.float32
                ) * (1.0 / HD**0.5)
                scores = jnp.where(live, scores, -1e30)
                expo = jnp.exp(scores - jnp.max(scores, axis=-1, keepdims=True))
                weights = (expo / jnp.sum(expo, axis=-1, keepdims=True)).astype(jnp.bfloat16)
                o_ref[s * TXT_S:(s + 1) * TXT_S, h * HD:(h + 1) * HD] = jnp.dot(
                    weights, values, preferred_element_type=jnp.float32
                ).astype(jnp.bfloat16)


def shards(image_rows, enc_gain, key_value_w, tiles, queries):
    dma = pltpu.SemaphoreType.DMA
    bf16, f32 = jnp.bfloat16, jnp.float32
    hbm = pl.BlockSpec(memory_space=pltpu.HBM)
    vmem = pl.BlockSpec(memory_space=pltpu.VMEM)
    parts = pl.pallas_call(
        project,
        out_shape=jax.ShapeDtypeStruct((2 * NX, IMG, 2 * HD), bf16),
        in_specs=[hbm, hbm, hbm],
        out_specs=hbm,
        scratch_shapes=[
            pltpu.VMEM((3 * IMG, 2048), bf16),
            pltpu.VMEM((2048,), bf16),
            pltpu.VMEM((NX, IMG, PART), bf16),
            pltpu.VMEM((NX * IMG, PART), bf16),
            pltpu.VMEM((NZ, PIECE, 1024), bf16),
            pltpu.VMEM((2, NX * IMG, 256), f32),
            pltpu.VMEM((2, NX * IMG, 256), f32),
            pltpu.VMEM((2, NX * IMG, 256), bf16),
            pltpu.VMEM((4, 8, 3 * IMG), f32),
            pltpu.VMEM((3, 8, IMG), f32),
            pltpu.VMEM((NX, 8, IMG), f32),
            dma((3,)),
            dma((3, NX)),
            dma((NX,)),
            dma((3,)),
            dma((3,)),
            dma((3, NX)),
            dma((NX,)),
            dma((2, 2)),
            dma((2, 2)),
            dma((2, 2, NZ)),
            dma((2, 2, NZ)),
            dma((2,)),
            dma((2,)),
            dma((2, NX)),
            dma((2 * NX,)),
            pltpu.SemaphoreType.REGULAR,
        ],
        compiler_params=pltpu.CompilerParams(
            collective_id=0, has_side_effects=True, vmem_limit_bytes=63 << 20
        ),
        name="project",
    )(image_rows, enc_gain, key_value_w)
    return pl.pallas_call(
        attend,
        out_shape=jax.ShapeDtypeStruct(queries.shape, bf16),
        in_specs=[pl.BlockSpec(memory_space=pltpu.SMEM), vmem, vmem],
        out_specs=vmem,
        compiler_params=pltpu.CompilerParams(vmem_limit_bytes=16 << 20),
        name="attend",
    )(tiles, parts, queries)


def solution(mesh):
    return jax.shard_map(
        shards,
        mesh=mesh,
        in_specs=(
            P(("grp", "fsdp"), "tp"),
            P("tp"),
            P(("tp", "fsdp"), None),
            P("fsdp"),
            P(("grp", "fsdp"), "tp"),
        ),
        out_specs=P(("grp", "fsdp"), "tp"),
        check_vma=False,
    )
```

```python
import jax
import jax.numpy as jnp
from jax import lax
from jax.experimental import pallas as pl
from jax.experimental.pallas import tpu as pltpu
from jax.sharding import PartitionSpec as P

D = 8192
HD = 128
KVH = 4
QH = 32
TILE_TOK = 16
SAMP = 2
TXT_S = 128
CAP = 64
IMG = 128
NX = 4
NZ = 16
FAR = 6
PIECE = 32
PART = 512
SPARE = 2
TURN = (2, 1, 3, 0)
MESH = pl.DeviceIdType.MESH


def project(
    rows_hbm, gain_hbm, w_hbm, out_ref,
    rows, gain_ref, inbox, normed, wz, mine, theirs, kept, packed, parts, half, stat, scale, scale_in,
    local_sem, rows_send, rows_recv, stat_send, stat_recv, scale_send, scale_recv,
    far_send, far_recv, near_send, near_recv, core_send, core_recv, half_send, half_recv, part_send, part_recv, ready,
):
    g = lax.axis_index("grp")
    f = lax.axis_index("fsdp")
    t = lax.axis_index("tp")
    x, z = f // NZ, f % NZ
    ylo, core = t // 2, t % 2

    def xs(step):
        return (x + step + NX) % NX

    def zs(step):
        return (z + step + NZ) % NZ

    def chip(gg, x1, z1, t1):
        return (gg, x1 * NZ + z1, t1)

    barrier = pltpu.get_barrier_semaphore()

    def hello(dev):
        pl.semaphore_signal(barrier, inc=1, device_id=dev, device_id_type=MESH)

    def copy(src, dst, ssem, rsem, dev):
        return pltpu.make_async_remote_copy(
            src_ref=src, dst_ref=dst, send_sem=ssem, recv_sem=rsem, device_id=dev, device_id_type=MESH
        )

    def got(dst, rsem):
        pltpu.make_async_copy(dst, dst, rsem).wait()

    def way(d):
        return 1 if d == 0 else -1

    @pl.when(g == SPARE)
    def _():
        pl.semaphore_wait(barrier, 4)

    @pl.when(g != SPARE)
    def _():
        own_w = pltpu.make_async_copy(w_hbm, wz.at[z], local_sem.at[0])
        own_gain = pltpu.make_async_copy(gain_hbm, gain_ref, local_sem.at[1])
        own_rows = pltpu.make_async_copy(rows_hbm, rows, local_sem.at[2])
        own_w.start()
        own_gain.start()
        for d in (1, -1, FAR, -FAR):
            hello(chip(g, x, zs(d), t))

        @pl.when(g == 0)
        def _():
            own_rows.start()
            for d in (1, 2, 3):
                hello((0, f, (t + d) % 4))
                hello(chip(0, xs(d), z, t))
            for gg in (1, 3):
                for xd in range(NX):
                    hello(chip(gg, xs(xd), z, t))
            for xd in range(NX):
                hello(chip(SPARE, xs(xd), z, (1 - ylo) * 2 + core))

        @pl.when(g > 0)
        def _():
            for xd in range(NX):
                hello(chip(0, xs(xd), z, t))
                hello(chip(g, xs(xd), z, (1 - ylo) * 2 + core))
            for xd in (1, 2, 3):
                hello(chip(g, xs(xd), z, t))
            hello((g, f, ylo * 2 + 1 - core))

        own_w.wait()
        own_gain.wait()

        @pl.when(g == 0)
        def _():
            pl.semaphore_wait(barrier, 18)

        @pl.when(g > 0)
        def _():
            pl.semaphore_wait(barrier, 16)

        sends = []

        def push(*a):
            c = copy(*a)
            c.start()
            sends.append(c)

        def cols(c):
            return pl.ds(c * PART, PART)

        def moved(o, d):
            return o - way(d)

        def cut(o, d):
            return pl.ds(16 * d, 16) if abs(o) == NZ // 2 else pl.ds(0, PIECE)

        def near(o, d, c):
            m = moved(o, d)
            ref = wz.at[zs(o), cut(m, d), cols(c)]
            push(ref, ref, near_send.at[d, c, m % NZ], near_recv.at[d, c, m % NZ], chip(g, x, zs(way(d)), t))

        def got_near(o, d, c):
            got(wz.at[zs(o), cut(o, d), cols(c)], near_recv.at[d, c, o % NZ])

        for c in (0, 1):
            for d in (0, 1):
                ref = wz.at[z, :, cols(c)]
                push(ref, ref, far_send.at[d, c], far_recv.at[d, c], chip(g, x, zs(FAR * way(d)), t))

        def rows_copy(i, gg, block, xd):
            src = rows_hbm.at[pl.ds(block * IMG, IMG), pl.ds(pl.multiple_of(xs(xd) * PART, PART), PART)]
            return copy(src, inbox.at[x], rows_send.at[i, xd], rows_recv.at[x], chip(gg, xs(xd), z, t))

        targets = ((1, 0), (3, 2), (0, 1))

        def own_inbox():
            src = rows_hbm.at[pl.ds(IMG, IMG), pl.ds(pl.multiple_of(x * PART, PART), PART)]
            return pltpu.make_async_copy(src, inbox.at[x], rows_recv.at[x])

        @pl.when(g == 0)
        def _():
            for xd in TURN:
                for i, (gg, block) in enumerate(targets):
                    if gg == 0 and xd == 0:
                        own_inbox().start()
                    else:
                        rows_copy(i, gg, block, xd).start()

        for c in (0, 1):
            for d in (0, 1):
                near(0, d, c)

        def stat_copy(d):
            return copy(stat.at[0], stat.at[d], stat_send.at[d - 1], stat_recv.at[d - 1], (0, f, (t + d) % 4))

        @pl.when(g == 0)
        def _():
            own_rows.wait()
            total = jnp.zeros((3 * IMG, 128), jnp.float32)
            for j in range(NZ):
                part = rows[:, j * 128:(j + 1) * 128].astype(jnp.float32)
                total = total + part * part
            line = jnp.sum(jnp.transpose(total), axis=0, keepdims=True)
            stat[0] = jnp.broadcast_to(line, (8, 3 * IMG))
            for d in (1, 2, 3):
                stat_copy(d).start()

        for c in (0, 1):
            for d in (0, 1):
                got_near(-way(d), d, c)
                near(-way(d), d, c)

        def scale_copy(i, gg, block, xd):
            return copy(
                scale.at[block], scale_in.at[x], scale_send.at[i, xd], scale_recv.at[x], chip(gg, xs(xd), z, t)
            )

        @pl.when(g == 0)
        def _():
            for d in (1, 2, 3):
                got(stat.at[d], stat_recv.at[d - 1])
            both = (stat[0] + stat[1]) + (stat[2] + stat[3])
            inv = lax.rsqrt(both / D + 1e-05)
            for block in range(3):
                scale[block] = inv[:, block * IMG:(block + 1) * IMG]
            for xd in range(NX):
                for i, (gg, block) in enumerate(targets):
                    if gg == 0 and xd == 0:
                        pltpu.make_async_copy(scale.at[block], scale_in.at[x], scale_recv.at[x]).start()
                    else:
                        scale_copy(i, gg, block, xd).start()

        for c in (0, 1):
            for d in (0, 1):
                got_near(-2 * way(d), d, c)
                near(-2 * way(d), d, c)
        for c in (0, 1):
            for d in (0, 1):
                got(wz.at[zs(-FAR * way(d)), :, cols(c)], far_recv.at[d, c])
            for d in (0, 1):
                near(-FAR * way(d), d, c)
                near(FAR * way(d), d, c)
        for c in (0, 1):
            for d in (0, 1):
                got_near(-7 * way(d), d, c)
                near(-7 * way(d), d, c)
                got_near(5 * way(d), d, c)
                near(5 * way(d), d, c)

        gains = []
        for j in range(PART // 128):
            pick = gain_ref[j * 128:(j + 1) * 128]
            for i in (1, 2, 3):
                pick = jnp.where(x == i, gain_ref[i * PART + j * 128:i * PART + (j + 1) * 128], pick)
            gains.append(pick.astype(jnp.float32).reshape(1, 128))
        for c in (0, 1):
            for d in (0, 1):
                got_near(-3 * way(d), d, c)
                got_near(-8 * way(d), d, c)
                got_near(4 * way(d), d, c)

        slot = x * 2 + ylo

        def side(j):
            return ylo if j == 0 else 1 - ylo

        def head(i, h):
            w = wz[:, :, pl.ds(pl.multiple_of(h * 256, 256), 256)].reshape(PART, 256)
            return jnp.dot(normed[i], w, preferred_element_type=jnp.float32)

        partner = (0, f, (1 - ylo) * 2 + core)

        def across(i):
            return copy(packed.at[i, 0], half.at[i], half_send.at[i], half_recv.at[i], partner)

        def part_copy(i, j, xd):
            gg = SPARE if j == 2 else g
            return copy(
                packed.at[i, min(j, 1)], parts.at[slot], part_send.at[min(j, 1), xd], part_recv.at[slot],
                chip(gg, xs(-xd), z, side(min(j, 1)) * 2 + core),
            )

        def begin(i, xd):
            src = xs(-xd)
            got(inbox.at[src], rows_recv.at[src])
            if i == 0:
                for k in range(NX):
                    got(scale_in.at[k], scale_recv.at[k])
            column = jnp.transpose(jnp.broadcast_to(scale_in[src, 0:1], (128, IMG)))
            for j in range(PART // 128):
                lanes = slice(j * 128, (j + 1) * 128)
                normed[i, :, lanes] = (
                    inbox[src, :, lanes].astype(jnp.float32) * column * gains[j]
                ).astype(jnp.bfloat16)
            for j in (0, 1):
                mine[i, j] = head(i, side(j) * 2 + 1 - core)
            push(mine.at[i], theirs.at[i], core_send.at[i], core_recv.at[i], (g, f, ylo * 2 + 1 - core))
            for j in (0, 1):
                kept[i, j] = head(i, side(j) * 2 + core)

        def finish(i, xd):
            got(theirs.at[i], core_recv.at[i])

            @pl.when(g == 0)
            def _():
                packed[i, 0] = (kept[i, 0] + theirs[i, 0]).astype(jnp.bfloat16)
                across(i).start()

            @pl.when(g > 0)
            def _():
                for j in (1, 0):
                    packed[i, j] = (kept[i, j] + theirs[i, j]).astype(jnp.bfloat16)
                    if j == 0 and xd == 0:
                        pltpu.make_async_copy(packed.at[i, j], parts.at[slot], part_recv.at[slot]).start()
                    else:
                        part_copy(i, j, xd).start()

        def final(i, xd):
            @pl.when(g == 0)
            def _():
                if i == 0:
                    pl.semaphore_wait(ready, 4)
                got(half.at[i], half_recv.at[i])
                packed[i, 1] = (
                    (kept[i, 1] + theirs[i, 1]) + half[i].astype(jnp.float32)
                ).astype(jnp.bfloat16)
                part_copy(i, 2, xd).start()

        for i in range(NX):
            begin(i, TURN[i])
            if i >= 1:
                finish(i - 1, TURN[i - 1])
            if i >= 2:
                final(i - 2, TURN[i - 2])
        finish(NX - 1, TURN[NX - 1])
        final(NX - 2, TURN[NX - 2])
        final(NX - 1, TURN[NX - 1])

        @pl.when(g > 0)
        def _():
            for i, xd in enumerate(TURN):
                for j in (1, 0):
                    if j == 1 or xd != 0:
                        part_copy(i, j, xd).wait_send()

        @pl.when(g == 0)
        def _():
            for i, xd in enumerate(TURN):
                across(i).wait_send()
                part_copy(i, 2, xd).wait_send()
            for d in (1, 2, 3):
                stat_copy(d).wait_send()
            for xd in range(NX):
                for i, (gg, block) in enumerate(targets):
                    if gg != 0 or xd != 0:
                        rows_copy(i, gg, block, xd).wait_send()
                        scale_copy(i, gg, block, xd).wait_send()

        for c in sends:
            c.wait_send()

    @pl.when(g == SPARE)
    def _():
        for xd in range(NX):
            pl.semaphore_signal(
                ready, inc=1, device_id=chip(0, xs(xd), z, (1 - ylo) * 2 + core), device_id_type=MESH
            )

    def gather_parts(slots):
        total = jnp.zeros((IMG, 2 * HD), jnp.float32)
        for i in slots:
            got(parts.at[i], part_recv.at[i])
            total = total + parts[i].astype(jnp.float32)
        out_ref[...] = total.astype(jnp.bfloat16)

    @pl.when(g == SPARE)
    def _():
        gather_parts([xs(-xd) * 2 + 1 - ylo for xd in TURN])

    @pl.when((g > 0) & (g != SPARE))
    def _():
        gather_parts(range(2 * NX))


def attend(tiles_ref, kv_ref, q_ref, o_ref):
    g = lax.axis_index("grp")

    @pl.when(g == 0)
    def _():
        o_ref[...] = jnp.zeros_like(o_ref)

    @pl.when(g > 0)
    def _():
        slot = lax.broadcasted_iota(jnp.int32, (TXT_S, CAP), 1)
        for s in range(SAMP):
            keys = kv_ref[s * CAP:(s + 1) * CAP, :HD]
            values = kv_ref[s * CAP:(s + 1) * CAP, HD:]
            live = slot < tiles_ref[(g - 1) * SAMP + s] * TILE_TOK
            for h in range(QH // KVH):
                q = q_ref[s * TXT_S:(s + 1) * TXT_S, h * HD:(h + 1) * HD]
                scores = lax.dot_general(
                    q, keys, (((1,), (1,)), ((), ())), preferred_element_type=jnp.float32
                ) * (1.0 / HD**0.5)
                scores = jnp.where(live, scores, -1e30)
                expo = jnp.exp(scores - jnp.max(scores, axis=-1, keepdims=True))
                weights = (expo / jnp.sum(expo, axis=-1, keepdims=True)).astype(jnp.bfloat16)
                o_ref[s * TXT_S:(s + 1) * TXT_S, h * HD:(h + 1) * HD] = jnp.dot(
                    weights, values, preferred_element_type=jnp.float32
                ).astype(jnp.bfloat16)


def shards(image_rows, enc_gain, key_value_w, tiles, queries):
    dma = pltpu.SemaphoreType.DMA
    bf16, f32 = jnp.bfloat16, jnp.float32
    hbm = pl.BlockSpec(memory_space=pltpu.HBM)
    vmem = pl.BlockSpec(memory_space=pltpu.VMEM)
    kv = pl.pallas_call(
        project,
        out_shape=jax.ShapeDtypeStruct((IMG, 2 * HD), bf16),
        in_specs=[hbm, hbm, hbm],
        out_specs=vmem,
        scratch_shapes=[
            pltpu.VMEM((3 * IMG, 2048), bf16),
            pltpu.VMEM((2048,), bf16),
            pltpu.VMEM((NX, IMG, PART), bf16),
            pltpu.VMEM((NX, IMG, PART), bf16),
            pltpu.VMEM((NZ, PIECE, 1024), bf16),
            pltpu.VMEM((NX, 2, IMG, 256), f32),
            pltpu.VMEM((NX, 2, IMG, 256), f32),
            pltpu.VMEM((NX, 2, IMG, 256), f32),
            pltpu.VMEM((NX, 2, IMG, 256), bf16),
            pltpu.VMEM((2 * NX, IMG, 256), bf16),
            pltpu.VMEM((NX, IMG, 256), bf16),
            pltpu.VMEM((4, 8, 3 * IMG), f32),
            pltpu.VMEM((3, 8, IMG), f32),
            pltpu.VMEM((NX, 8, IMG), f32),
            dma((3,)),
            dma((3, NX)),
            dma((NX,)),
            dma((3,)),
            dma((3,)),
            dma((3, NX)),
            dma((NX,)),
            dma((2, 2)),
            dma((2, 2)),
            dma((2, 2, NZ)),
            dma((2, 2, NZ)),
            dma((NX,)),
            dma((NX,)),
            dma((NX,)),
            dma((NX,)),
            dma((2, NX)),
            dma((2 * NX,)),
            pltpu.SemaphoreType.REGULAR,
        ],
        compiler_params=pltpu.CompilerParams(
            collective_id=0, has_side_effects=True, vmem_limit_bytes=63 << 20
        ),
        name="project",
    )(image_rows, enc_gain, key_value_w)
    return pl.pallas_call(
        attend,
        out_shape=jax.ShapeDtypeStruct(queries.shape, bf16),
        in_specs=[pl.BlockSpec(memory_space=pltpu.SMEM), vmem, vmem],
        out_specs=vmem,
        compiler_params=pltpu.CompilerParams(vmem_limit_bytes=16 << 20),
        name="attend",
    )(tiles, kv, queries)


def solution(mesh):
    return jax.shard_map(
        shards,
        mesh=mesh,
        in_specs=(
            P(("grp", "fsdp"), "tp"),
            P("tp"),
            P(("tp", "fsdp"), None),
            P("fsdp"),
            P(("grp", "fsdp"), "tp"),
        ),
        out_specs=P(("grp", "fsdp"), "tp"),
        check_vma=False,
    )
```

```python
import jax
import jax.numpy as jnp
from jax import lax
from jax.experimental import pallas as pl
from jax.experimental.pallas import tpu as pltpu
from jax.sharding import PartitionSpec as P

D = 8192
HD = 128
KVH = 4
QH = 32
TILE_TOK = 16
SAMP = 2
TXT_S = 128
CAP = 64
IMG = 128
NX = 4
NZ = 16
FAR = 6
PIECE = 32
PART = 512
SPARE = 2
TURN = (2, 1, 3, 0)
MESH = pl.DeviceIdType.MESH


def project(
    rows_hbm, gain_hbm, w_hbm, out_ref,
    rows, gain_ref, inbox, normed, wz, mine, theirs, kept, packed, parts, half, stat, scale, scale_in,
    local_sem, rows_send, rows_recv, stat_send, stat_recv, scale_send, scale_recv,
    far_send, far_recv, near_send, near_recv, core_send, core_recv, half_send, half_recv, part_send, part_recv, ready,
):
    g = lax.axis_index("grp")
    f = lax.axis_index("fsdp")
    t = lax.axis_index("tp")
    x, z = f // NZ, f % NZ
    ylo, core = t // 2, t % 2

    def xs(step):
        return (x + step + NX) % NX

    def zs(step):
        return (z + step + NZ) % NZ

    def chip(gg, x1, z1, t1):
        return (gg, x1 * NZ + z1, t1)

    barrier = pltpu.get_barrier_semaphore()

    def hello(dev):
        pl.semaphore_signal(barrier, inc=1, device_id=dev, device_id_type=MESH)

    def copy(src, dst, ssem, rsem, dev):
        return pltpu.make_async_remote_copy(
            src_ref=src, dst_ref=dst, send_sem=ssem, recv_sem=rsem, device_id=dev, device_id_type=MESH
        )

    def got(dst, rsem):
        pltpu.make_async_copy(dst, dst, rsem).wait()

    def way(d):
        return 1 if d == 0 else -1

    @pl.when(g == SPARE)
    def _():
        pl.semaphore_wait(barrier, 4)

    @pl.when(g != SPARE)
    def _():
        own_w = pltpu.make_async_copy(w_hbm, wz.at[z], local_sem.at[0])
        own_gain = pltpu.make_async_copy(gain_hbm, gain_ref, local_sem.at[1])
        own_rows = pltpu.make_async_copy(rows_hbm, rows, local_sem.at[2])
        own_w.start()
        own_gain.start()
        for d in (1, -1, FAR, -FAR):
            hello(chip(g, x, zs(d), t))

        @pl.when(g == 0)
        def _():
            own_rows.start()
            for d in (1, 2, 3):
                hello((0, f, (t + d) % 4))
                hello(chip(0, xs(d), z, t))
            for gg in (1, 3):
                for xd in range(NX):
                    hello(chip(gg, xs(xd), z, t))
            for xd in range(NX):
                hello(chip(SPARE, xs(xd), z, (1 - ylo) * 2 + core))

        @pl.when(g > 0)
        def _():
            for xd in range(NX):
                hello(chip(0, xs(xd), z, t))
                hello(chip(g, xs(xd), z, (1 - ylo) * 2 + core))
            for xd in (1, 2, 3):
                hello(chip(g, xs(xd), z, t))
            hello((g, f, ylo * 2 + 1 - core))

        own_w.wait()
        own_gain.wait()

        @pl.when(g == 0)
        def _():
            pl.semaphore_wait(barrier, 18)

        @pl.when(g > 0)
        def _():
            pl.semaphore_wait(barrier, 16)

        sends = []

        def push(*a):
            c = copy(*a)
            c.start()
            sends.append(c)

        def cols(c):
            return pl.ds(c * PART, PART)

        def moved(o, d):
            return o - way(d)

        def cut(o, d):
            return pl.ds(16 * d, 16) if abs(o) == NZ // 2 else pl.ds(0, PIECE)

        def near(o, d, c):
            m = moved(o, d)
            ref = wz.at[zs(o), cut(m, d), cols(c)]
            push(ref, ref, near_send.at[d, c, m % NZ], near_recv.at[d, c, m % NZ], chip(g, x, zs(way(d)), t))

        def got_near(o, d, c):
            got(wz.at[zs(o), cut(o, d), cols(c)], near_recv.at[d, c, o % NZ])

        for c in (0, 1):
            for d in (0, 1):
                ref = wz.at[z, :, cols(c)]
                push(ref, ref, far_send.at[d, c], far_recv.at[d, c], chip(g, x, zs(FAR * way(d)), t))

        def rows_copy(i, gg, block, xd):
            src = rows_hbm.at[pl.ds(block * IMG, IMG), pl.ds(pl.multiple_of(xs(xd) * PART, PART), PART)]
            return copy(src, inbox.at[x], rows_send.at[i, xd], rows_recv.at[x], chip(gg, xs(xd), z, t))

        targets = ((1, 0), (3, 2), (0, 1))

        def own_inbox():
            src = rows_hbm.at[pl.ds(IMG, IMG), pl.ds(pl.multiple_of(x * PART, PART), PART)]
            return pltpu.make_async_copy(src, inbox.at[x], rows_recv.at[x])

        @pl.when(g == 0)
        def _():
            own_inbox().start()
            for xd in TURN[:3]:
                rows_copy(2, 0, 1, xd).start()
            for xd in TURN:
                for i, (gg, block) in enumerate(targets[:2]):
                    rows_copy(i, gg, block, xd).start()

        for c in (0, 1):
            for d in (0, 1):
                near(0, d, c)

        def stat_copy(d):
            return copy(stat.at[0], stat.at[d], stat_send.at[d - 1], stat_recv.at[d - 1], (0, f, (t + d) % 4))

        @pl.when(g == 0)
        def _():
            own_rows.wait()
            total = jnp.zeros((3 * IMG, 128), jnp.float32)
            for j in range(NZ):
                part = rows[:, j * 128:(j + 1) * 128].astype(jnp.float32)
                total = total + part * part
            line = jnp.sum(jnp.transpose(total), axis=0, keepdims=True)
            stat[0] = jnp.broadcast_to(line, (8, 3 * IMG))
            for d in (1, 2, 3):
                stat_copy(d).start()

        for c in (0, 1):
            for d in (0, 1):
                got_near(-way(d), d, c)
                near(-way(d), d, c)

        def scale_copy(i, gg, block, xd):
            return copy(
                scale.at[block], scale_in.at[x], scale_send.at[i, xd], scale_recv.at[x], chip(gg, xs(xd), z, t)
            )

        @pl.when(g == 0)
        def _():
            for d in (1, 2, 3):
                got(stat.at[d], stat_recv.at[d - 1])
            both = (stat[0] + stat[1]) + (stat[2] + stat[3])
            inv = lax.rsqrt(both / D + 1e-05)
            for block in range(3):
                scale[block] = inv[:, block * IMG:(block + 1) * IMG]
            for xd in range(NX):
                for i, (gg, block) in enumerate(targets):
                    if gg == 0 and xd == 0:
                        pltpu.make_async_copy(scale.at[block], scale_in.at[x], scale_recv.at[x]).start()
                    else:
                        scale_copy(i, gg, block, xd).start()

        for c in (0, 1):
            for d in (0, 1):
                got(wz.at[zs(-FAR * way(d)), :, cols(c)], far_recv.at[d, c])
            for d in (0, 1):
                near(-FAR * way(d), d, c)
                near(FAR * way(d), d, c)
        for c in (0, 1):
            for d in (0, 1):
                got_near(-2 * way(d), d, c)
                near(-2 * way(d), d, c)
        for c in (0, 1):
            for d in (0, 1):
                got_near(-7 * way(d), d, c)
                near(-7 * way(d), d, c)
                got_near(5 * way(d), d, c)
                near(5 * way(d), d, c)

        gains = []
        for j in range(PART // 128):
            pick = gain_ref[j * 128:(j + 1) * 128]
            for i in (1, 2, 3):
                pick = jnp.where(x == i, gain_ref[i * PART + j * 128:i * PART + (j + 1) * 128], pick)
            gains.append(pick.astype(jnp.float32).reshape(1, 128))
        for c in (0, 1):
            for d in (0, 1):
                got_near(-3 * way(d), d, c)
                got_near(-8 * way(d), d, c)
                got_near(4 * way(d), d, c)

        slot = x * 2 + ylo

        def side(j):
            return ylo if j == 0 else 1 - ylo

        def head(i, h):
            w = wz[:, :, pl.ds(pl.multiple_of(h * 256, 256), 256)].reshape(PART, 256)
            return jnp.dot(normed[i], w, preferred_element_type=jnp.float32)

        partner = (0, f, (1 - ylo) * 2 + core)

        def across(i):
            return copy(packed.at[i, 0], half.at[i], half_send.at[i], half_recv.at[i], partner)

        def part_copy(i, j, xd):
            gg = SPARE if j == 2 else g
            return copy(
                packed.at[i, min(j, 1)], parts.at[slot], part_send.at[min(j, 1), xd], part_recv.at[slot],
                chip(gg, xs(-xd), z, side(min(j, 1)) * 2 + core),
            )

        def begin(i, xd):
            src = xs(-xd)
            got(inbox.at[src], rows_recv.at[src])
            if i == 0:
                for k in range(NX):
                    got(scale_in.at[k], scale_recv.at[k])
            column = jnp.transpose(jnp.broadcast_to(scale_in[src, 0:1], (128, IMG)))
            for j in range(PART // 128):
                lanes = slice(j * 128, (j + 1) * 128)
                normed[i, :, lanes] = (
                    inbox[src, :, lanes].astype(jnp.float32) * column * gains[j]
                ).astype(jnp.bfloat16)
            for j in (0, 1):
                mine[i, j] = head(i, side(j) * 2 + 1 - core)
            push(mine.at[i], theirs.at[i], core_send.at[i], core_recv.at[i], (g, f, ylo * 2 + 1 - core))
            for j in (0, 1):
                kept[i, j] = head(i, side(j) * 2 + core)

        def finish(i, xd):
            got(theirs.at[i], core_recv.at[i])

            @pl.when(g == 0)
            def _():
                packed[i, 0] = (kept[i, 0] + theirs[i, 0]).astype(jnp.bfloat16)
                across(i).start()

            @pl.when(g > 0)
            def _():
                for j in (1, 0):
                    packed[i, j] = (kept[i, j] + theirs[i, j]).astype(jnp.bfloat16)
                    if j == 0 and xd == 0:
                        pltpu.make_async_copy(packed.at[i, j], parts.at[slot], part_recv.at[slot]).start()
                    else:
                        part_copy(i, j, xd).start()

        def final(i, xd):
            @pl.when(g == 0)
            def _():
                if i == 0:
                    pl.semaphore_wait(ready, 4)
                got(half.at[i], half_recv.at[i])
                packed[i, 1] = (
                    (kept[i, 1] + theirs[i, 1]) + half[i].astype(jnp.float32)
                ).astype(jnp.bfloat16)
                part_copy(i, 2, xd).start()

        for i in range(NX):
            begin(i, TURN[i])
            if i >= 1:
                finish(i - 1, TURN[i - 1])
            if i >= 2:
                final(i - 2, TURN[i - 2])
        finish(NX - 1, TURN[NX - 1])
        final(NX - 2, TURN[NX - 2])
        final(NX - 1, TURN[NX - 1])

        @pl.when(g > 0)
        def _():
            for i, xd in enumerate(TURN):
                for j in (1, 0):
                    if j == 1 or xd != 0:
                        part_copy(i, j, xd).wait_send()

        @pl.when(g == 0)
        def _():
            for i, xd in enumerate(TURN):
                across(i).wait_send()
                part_copy(i, 2, xd).wait_send()
            for d in (1, 2, 3):
                stat_copy(d).wait_send()
            for xd in range(NX):
                for i, (gg, block) in enumerate(targets):
                    if gg != 0 or xd != 0:
                        rows_copy(i, gg, block, xd).wait_send()
                        scale_copy(i, gg, block, xd).wait_send()

        for c in sends:
            c.wait_send()

    @pl.when(g == SPARE)
    def _():
        for xd in range(NX):
            pl.semaphore_signal(
                ready, inc=1, device_id=chip(0, xs(xd), z, (1 - ylo) * 2 + core), device_id_type=MESH
            )

    def gather_parts(slots):
        total = jnp.zeros((IMG, 2 * HD), jnp.float32)
        for i in slots:
            got(parts.at[i], part_recv.at[i])
            total = total + parts[i].astype(jnp.float32)
        out_ref[...] = total.astype(jnp.bfloat16)

    @pl.when(g == SPARE)
    def _():
        gather_parts([xs(-xd) * 2 + 1 - ylo for xd in TURN])

    @pl.when((g > 0) & (g != SPARE))
    def _():
        gather_parts(range(2 * NX))


def attend(tiles_ref, kv_ref, q_ref, o_ref):
    g = lax.axis_index("grp")

    @pl.when(g == 0)
    def _():
        o_ref[...] = jnp.zeros_like(o_ref)

    @pl.when(g > 0)
    def _():
        slot = lax.broadcasted_iota(jnp.int32, (TXT_S, CAP), 1)
        for s in range(SAMP):
            keys = kv_ref[s * CAP:(s + 1) * CAP, :HD]
            values = kv_ref[s * CAP:(s + 1) * CAP, HD:]
            live = slot < tiles_ref[(g - 1) * SAMP + s] * TILE_TOK
            for h in range(QH // KVH):
                q = q_ref[s * TXT_S:(s + 1) * TXT_S, h * HD:(h + 1) * HD]
                scores = lax.dot_general(
                    q, keys, (((1,), (1,)), ((), ())), preferred_element_type=jnp.float32
                ) * (1.0 / HD**0.5)
                scores = jnp.where(live, scores, -1e30)
                expo = jnp.exp(scores - jnp.max(scores, axis=-1, keepdims=True))
                weights = (expo / jnp.sum(expo, axis=-1, keepdims=True)).astype(jnp.bfloat16)
                o_ref[s * TXT_S:(s + 1) * TXT_S, h * HD:(h + 1) * HD] = jnp.dot(
                    weights, values, preferred_element_type=jnp.float32
                ).astype(jnp.bfloat16)


def shards(image_rows, enc_gain, key_value_w, tiles, queries):
    dma = pltpu.SemaphoreType.DMA
    bf16, f32 = jnp.bfloat16, jnp.float32
    hbm = pl.BlockSpec(memory_space=pltpu.HBM)
    vmem = pl.BlockSpec(memory_space=pltpu.VMEM)
    kv = pl.pallas_call(
        project,
        out_shape=jax.ShapeDtypeStruct((IMG, 2 * HD), bf16),
        in_specs=[hbm, hbm, hbm],
        out_specs=vmem,
        scratch_shapes=[
            pltpu.VMEM((3 * IMG, 2048), bf16),
            pltpu.VMEM((2048,), bf16),
            pltpu.VMEM((NX, IMG, PART), bf16),
            pltpu.VMEM((NX, IMG, PART), bf16),
            pltpu.VMEM((NZ, PIECE, 1024), bf16),
            pltpu.VMEM((NX, 2, IMG, 256), f32),
            pltpu.VMEM((NX, 2, IMG, 256), f32),
            pltpu.VMEM((NX, 2, IMG, 256), f32),
            pltpu.VMEM((NX, 2, IMG, 256), bf16),
            pltpu.VMEM((2 * NX, IMG, 256), bf16),
            pltpu.VMEM((NX, IMG, 256), bf16),
            pltpu.VMEM((4, 8, 3 * IMG), f32),
            pltpu.VMEM((3, 8, IMG), f32),
            pltpu.VMEM((NX, 8, IMG), f32),
            dma((3,)),
            dma((3, NX)),
            dma((NX,)),
            dma((3,)),
            dma((3,)),
            dma((3, NX)),
            dma((NX,)),
            dma((2, 2)),
            dma((2, 2)),
            dma((2, 2, NZ)),
            dma((2, 2, NZ)),
            dma((NX,)),
            dma((NX,)),
            dma((NX,)),
            dma((NX,)),
            dma((2, NX)),
            dma((2 * NX,)),
            pltpu.SemaphoreType.REGULAR,
        ],
        compiler_params=pltpu.CompilerParams(
            collective_id=0, has_side_effects=True, vmem_limit_bytes=63 << 20
        ),
        name="project",
    )(image_rows, enc_gain, key_value_w)
    return pl.pallas_call(
        attend,
        out_shape=jax.ShapeDtypeStruct(queries.shape, bf16),
        in_specs=[pl.BlockSpec(memory_space=pltpu.SMEM), vmem, vmem],
        out_specs=vmem,
        compiler_params=pltpu.CompilerParams(vmem_limit_bytes=16 << 20),
        name="attend",
    )(tiles, kv, queries)


def solution(mesh):
    return jax.shard_map(
        shards,
        mesh=mesh,
        in_specs=(
            P(("grp", "fsdp"), "tp"),
            P("tp"),
            P(("tp", "fsdp"), None),
            P("fsdp"),
            P(("grp", "fsdp"), "tp"),
        ),
        out_specs=P(("grp", "fsdp"), "tp"),
        check_vma=False,
    )
```

```python
import jax
import jax.numpy as jnp
from jax import lax
from jax.experimental import pallas as pl
from jax.experimental.pallas import tpu as pltpu
from jax.sharding import PartitionSpec as P

D = 8192
HD = 128
KVH = 4
QH = 32
TILE_TOK = 16
SAMP = 2
TXT_S = 128
CAP = 64
IMG = 128
NX = 4
NZ = 16
FAR = 6
PIECE = 32
PART = 512
SPARE = 2
TURN = (2, 1, 3, 0)
MESH = pl.DeviceIdType.MESH


def project(
    rows_hbm, gain_hbm, w_hbm, out_ref,
    rows, gain_ref, inbox, normed, wz, mine, theirs, kept, packed, parts, half, stat, scale, scale_in,
    local_sem, rows_send, rows_recv, stat_send, stat_recv, scale_send, scale_recv,
    far_send, far_recv, near_send, near_recv, core_send, core_recv, half_send, half_recv, part_send, part_recv, ready,
):
    g = lax.axis_index("grp")
    f = lax.axis_index("fsdp")
    t = lax.axis_index("tp")
    x, z = f // NZ, f % NZ
    ylo, core = t // 2, t % 2

    def xs(step):
        return (x + step + NX) % NX

    def zs(step):
        return (z + step + NZ) % NZ

    def chip(gg, x1, z1, t1):
        return (gg, x1 * NZ + z1, t1)

    barrier = pltpu.get_barrier_semaphore()

    def hello(dev):
        pl.semaphore_signal(barrier, inc=1, device_id=dev, device_id_type=MESH)

    def copy(src, dst, ssem, rsem, dev):
        return pltpu.make_async_remote_copy(
            src_ref=src, dst_ref=dst, send_sem=ssem, recv_sem=rsem, device_id=dev, device_id_type=MESH
        )

    def got(dst, rsem):
        pltpu.make_async_copy(dst, dst, rsem).wait()

    def way(d):
        return 1 if d == 0 else -1

    @pl.when(g == SPARE)
    def _():
        pl.semaphore_wait(barrier, 4)

    @pl.when(g != SPARE)
    def _():
        own_w = pltpu.make_async_copy(w_hbm, wz.at[z], local_sem.at[0])
        own_gain = pltpu.make_async_copy(gain_hbm, gain_ref, local_sem.at[1])
        own_rows = pltpu.make_async_copy(rows_hbm, rows, local_sem.at[2])
        own_w.start()
        own_gain.start()
        for d in (1, -1, FAR, -FAR):
            hello(chip(g, x, zs(d), t))

        @pl.when(g == 0)
        def _():
            own_rows.start()
            for d in (1, 2, 3):
                hello((0, f, (t + d) % 4))
                hello(chip(0, xs(d), z, t))
            for gg in (1, 3):
                for xd in range(NX):
                    hello(chip(gg, xs(xd), z, t))
            for xd in range(NX):
                hello(chip(SPARE, xs(xd), z, (1 - ylo) * 2 + core))

        @pl.when(g > 0)
        def _():
            for xd in range(NX):
                hello(chip(0, xs(xd), z, t))
                hello(chip(g, xs(xd), z, (1 - ylo) * 2 + core))
            for xd in (1, 2, 3):
                hello(chip(g, xs(xd), z, t))
            hello((g, f, ylo * 2 + 1 - core))

        own_w.wait()
        own_gain.wait()

        @pl.when(g == 0)
        def _():
            pl.semaphore_wait(barrier, 18)

        @pl.when(g > 0)
        def _():
            pl.semaphore_wait(barrier, 16)

        sends = []

        def push(*a):
            c = copy(*a)
            c.start()
            sends.append(c)

        def cols(c):
            return pl.ds(c * PART, PART)

        def moved(o, d):
            return o - way(d)

        def cut(o, d):
            return pl.ds(16 * d, 16) if abs(o) == NZ // 2 else pl.ds(0, PIECE)

        def near(o, d, c):
            m = moved(o, d)
            ref = wz.at[zs(o), cut(m, d), cols(c)]
            push(ref, ref, near_send.at[d, c, m % NZ], near_recv.at[d, c, m % NZ], chip(g, x, zs(way(d)), t))

        def got_near(o, d, c):
            got(wz.at[zs(o), cut(o, d), cols(c)], near_recv.at[d, c, o % NZ])

        for c in (0, 1):
            for d in (0, 1):
                ref = wz.at[z, :, cols(c)]
                push(ref, ref, far_send.at[d, c], far_recv.at[d, c], chip(g, x, zs(FAR * way(d)), t))

        def rows_copy(i, gg, block, xd):
            src = rows_hbm.at[pl.ds(block * IMG, IMG), pl.ds(pl.multiple_of(xs(xd) * PART, PART), PART)]
            return copy(src, inbox.at[x], rows_send.at[i, xd], rows_recv.at[x], chip(gg, xs(xd), z, t))

        targets = ((1, 0), (3, 2), (0, 1))

        def own_inbox():
            src = rows_hbm.at[pl.ds(IMG, IMG), pl.ds(pl.multiple_of(x * PART, PART), PART)]
            return pltpu.make_async_copy(src, inbox.at[x], rows_recv.at[x])

        @pl.when(g == 0)
        def _():
            own_inbox().start()
            for xd in TURN[:3]:
                rows_copy(2, 0, 1, xd).start()
            for xd in TURN:
                for i, (gg, block) in enumerate(targets[:2]):
                    rows_copy(i, gg, block, xd).start()

        for c in (0, 1):
            for d in (0, 1):
                near(0, d, c)

        def stat_copy(d):
            return copy(stat.at[0], stat.at[d], stat_send.at[d - 1], stat_recv.at[d - 1], (0, f, (t + d) % 4))

        for c in (0, 1):
            for d in (0, 1):
                got_near(-way(d), d, c)
                near(-way(d), d, c)

        @pl.when(g == 0)
        def _():
            own_rows.wait()
            total = jnp.zeros((3 * IMG, 128), jnp.float32)
            for j in range(NZ):
                part = rows[:, j * 128:(j + 1) * 128].astype(jnp.float32)
                total = total + part * part
            line = jnp.sum(jnp.transpose(total), axis=0, keepdims=True)
            stat[0] = jnp.broadcast_to(line, (8, 3 * IMG))
            for d in (1, 2, 3):
                stat_copy(d).start()

        def scale_copy(i, gg, block, xd):
            return copy(
                scale.at[block], scale_in.at[x], scale_send.at[i, xd], scale_recv.at[x], chip(gg, xs(xd), z, t)
            )

        for c in (0, 1):
            for d in (0, 1):
                got(wz.at[zs(-FAR * way(d)), :, cols(c)], far_recv.at[d, c])
            for d in (0, 1):
                near(-FAR * way(d), d, c)
                near(FAR * way(d), d, c)
        @pl.when(g == 0)
        def _():
            for d in (1, 2, 3):
                got(stat.at[d], stat_recv.at[d - 1])
            both = (stat[0] + stat[1]) + (stat[2] + stat[3])
            inv = lax.rsqrt(both / D + 1e-05)
            for block in range(3):
                scale[block] = inv[:, block * IMG:(block + 1) * IMG]
            for xd in range(NX):
                for i, (gg, block) in enumerate(targets):
                    if gg == 0 and xd == 0:
                        pltpu.make_async_copy(scale.at[block], scale_in.at[x], scale_recv.at[x]).start()
                    else:
                        scale_copy(i, gg, block, xd).start()

        for c in (0, 1):
            for d in (0, 1):
                got_near(-2 * way(d), d, c)
                near(-2 * way(d), d, c)
        for c in (0, 1):
            for d in (0, 1):
                got_near(-7 * way(d), d, c)
                near(-7 * way(d), d, c)
                got_near(5 * way(d), d, c)
                near(5 * way(d), d, c)

        gains = []
        for j in range(PART // 128):
            pick = gain_ref[j * 128:(j + 1) * 128]
            for i in (1, 2, 3):
                pick = jnp.where(x == i, gain_ref[i * PART + j * 128:i * PART + (j + 1) * 128], pick)
            gains.append(pick.astype(jnp.float32).reshape(1, 128))
        for c in (0, 1):
            for d in (0, 1):
                got_near(-3 * way(d), d, c)
                got_near(-8 * way(d), d, c)
                got_near(4 * way(d), d, c)

        slot = x * 2 + ylo

        def side(j):
            return ylo if j == 0 else 1 - ylo

        def head(i, h):
            w = wz[:, :, pl.ds(pl.multiple_of(h * 256, 256), 256)].reshape(PART, 256)
            return jnp.dot(normed[i], w, preferred_element_type=jnp.float32)

        partner = (0, f, (1 - ylo) * 2 + core)

        def across(i):
            return copy(packed.at[i, 0], half.at[i], half_send.at[i], half_recv.at[i], partner)

        def part_copy(i, j, xd):
            gg = SPARE if j == 2 else g
            return copy(
                packed.at[i, min(j, 1)], parts.at[slot], part_send.at[min(j, 1), xd], part_recv.at[slot],
                chip(gg, xs(-xd), z, side(min(j, 1)) * 2 + core),
            )

        def begin(i, xd):
            src = xs(-xd)
            got(inbox.at[src], rows_recv.at[src])
            if i == 0:
                for k in range(NX):
                    got(scale_in.at[k], scale_recv.at[k])
            column = jnp.transpose(jnp.broadcast_to(scale_in[src, 0:1], (128, IMG)))
            for j in range(PART // 128):
                lanes = slice(j * 128, (j + 1) * 128)
                normed[i, :, lanes] = (
                    inbox[src, :, lanes].astype(jnp.float32) * column * gains[j]
                ).astype(jnp.bfloat16)
            for j in (0, 1):
                mine[i, j] = head(i, side(j) * 2 + 1 - core)
            push(mine.at[i], theirs.at[i], core_send.at[i], core_recv.at[i], (g, f, ylo * 2 + 1 - core))
            for j in (0, 1):
                kept[i, j] = head(i, side(j) * 2 + core)

        def finish(i, xd):
            got(theirs.at[i], core_recv.at[i])

            @pl.when(g == 0)
            def _():
                packed[i, 0] = (kept[i, 0] + theirs[i, 0]).astype(jnp.bfloat16)
                across(i).start()

            @pl.when(g > 0)
            def _():
                for j in (1, 0):
                    packed[i, j] = (kept[i, j] + theirs[i, j]).astype(jnp.bfloat16)
                    if j == 0 and xd == 0:
                        pltpu.make_async_copy(packed.at[i, j], parts.at[slot], part_recv.at[slot]).start()
                    else:
                        part_copy(i, j, xd).start()

        def final(i, xd):
            @pl.when(g == 0)
            def _():
                if i == 0:
                    pl.semaphore_wait(ready, 4)
                got(half.at[i], half_recv.at[i])
                packed[i, 1] = (
                    (kept[i, 1] + theirs[i, 1]) + half[i].astype(jnp.float32)
                ).astype(jnp.bfloat16)
                part_copy(i, 2, xd).start()

        for i in range(NX):
            begin(i, TURN[i])
            if i >= 1:
                finish(i - 1, TURN[i - 1])
            if i >= 2:
                final(i - 2, TURN[i - 2])
        finish(NX - 1, TURN[NX - 1])
        final(NX - 2, TURN[NX - 2])
        final(NX - 1, TURN[NX - 1])

        @pl.when(g > 0)
        def _():
            for i, xd in enumerate(TURN):
                for j in (1, 0):
                    if j == 1 or xd != 0:
                        part_copy(i, j, xd).wait_send()

        @pl.when(g == 0)
        def _():
            for i, xd in enumerate(TURN):
                across(i).wait_send()
                part_copy(i, 2, xd).wait_send()
            for d in (1, 2, 3):
                stat_copy(d).wait_send()
            for xd in range(NX):
                for i, (gg, block) in enumerate(targets):
                    if gg != 0 or xd != 0:
                        rows_copy(i, gg, block, xd).wait_send()
                        scale_copy(i, gg, block, xd).wait_send()

        for c in sends:
            c.wait_send()

    @pl.when(g == SPARE)
    def _():
        for xd in range(NX):
            pl.semaphore_signal(
                ready, inc=1, device_id=chip(0, xs(xd), z, (1 - ylo) * 2 + core), device_id_type=MESH
            )

    def gather_parts(slots):
        total = jnp.zeros((IMG, 2 * HD), jnp.float32)
        for i in slots:
            got(parts.at[i], part_recv.at[i])
            total = total + parts[i].astype(jnp.float32)
        out_ref[...] = total.astype(jnp.bfloat16)

    @pl.when(g == SPARE)
    def _():
        gather_parts([xs(-xd) * 2 + 1 - ylo for xd in TURN])

    @pl.when((g > 0) & (g != SPARE))
    def _():
        gather_parts(range(2 * NX))


def attend(tiles_ref, kv_ref, q_ref, o_ref):
    g = lax.axis_index("grp")

    @pl.when(g == 0)
    def _():
        o_ref[...] = jnp.zeros_like(o_ref)

    @pl.when(g > 0)
    def _():
        slot = lax.broadcasted_iota(jnp.int32, (TXT_S, CAP), 1)
        for s in range(SAMP):
            keys = kv_ref[s * CAP:(s + 1) * CAP, :HD]
            values = kv_ref[s * CAP:(s + 1) * CAP, HD:]
            live = slot < tiles_ref[(g - 1) * SAMP + s] * TILE_TOK
            for h in range(QH // KVH):
                q = q_ref[s * TXT_S:(s + 1) * TXT_S, h * HD:(h + 1) * HD]
                scores = lax.dot_general(
                    q, keys, (((1,), (1,)), ((), ())), preferred_element_type=jnp.float32
                ) * (1.0 / HD**0.5)
                scores = jnp.where(live, scores, -1e30)
                expo = jnp.exp(scores - jnp.max(scores, axis=-1, keepdims=True))
                weights = (expo / jnp.sum(expo, axis=-1, keepdims=True)).astype(jnp.bfloat16)
                o_ref[s * TXT_S:(s + 1) * TXT_S, h * HD:(h + 1) * HD] = jnp.dot(
                    weights, values, preferred_element_type=jnp.float32
                ).astype(jnp.bfloat16)


def shards(image_rows, enc_gain, key_value_w, tiles, queries):
    dma = pltpu.SemaphoreType.DMA
    bf16, f32 = jnp.bfloat16, jnp.float32
    hbm = pl.BlockSpec(memory_space=pltpu.HBM)
    vmem = pl.BlockSpec(memory_space=pltpu.VMEM)
    kv = pl.pallas_call(
        project,
        out_shape=jax.ShapeDtypeStruct((IMG, 2 * HD), bf16),
        in_specs=[hbm, hbm, hbm],
        out_specs=vmem,
        scratch_shapes=[
            pltpu.VMEM((3 * IMG, 2048), bf16),
            pltpu.VMEM((2048,), bf16),
            pltpu.VMEM((NX, IMG, PART), bf16),
            pltpu.VMEM((NX, IMG, PART), bf16),
            pltpu.VMEM((NZ, PIECE, 1024), bf16),
            pltpu.VMEM((NX, 2, IMG, 256), f32),
            pltpu.VMEM((NX, 2, IMG, 256), f32),
            pltpu.VMEM((NX, 2, IMG, 256), f32),
            pltpu.VMEM((NX, 2, IMG, 256), bf16),
            pltpu.VMEM((2 * NX, IMG, 256), bf16),
            pltpu.VMEM((NX, IMG, 256), bf16),
            pltpu.VMEM((4, 8, 3 * IMG), f32),
            pltpu.VMEM((3, 8, IMG), f32),
            pltpu.VMEM((NX, 8, IMG), f32),
            dma((3,)),
            dma((3, NX)),
            dma((NX,)),
            dma((3,)),
            dma((3,)),
            dma((3, NX)),
            dma((NX,)),
            dma((2, 2)),
            dma((2, 2)),
            dma((2, 2, NZ)),
            dma((2, 2, NZ)),
            dma((NX,)),
            dma((NX,)),
            dma((NX,)),
            dma((NX,)),
            dma((2, NX)),
            dma((2 * NX,)),
            pltpu.SemaphoreType.REGULAR,
        ],
        compiler_params=pltpu.CompilerParams(
            collective_id=0, has_side_effects=True, vmem_limit_bytes=63 << 20
        ),
        name="project",
    )(image_rows, enc_gain, key_value_w)
    return pl.pallas_call(
        attend,
        out_shape=jax.ShapeDtypeStruct(queries.shape, bf16),
        in_specs=[pl.BlockSpec(memory_space=pltpu.SMEM), vmem, vmem],
        out_specs=vmem,
        compiler_params=pltpu.CompilerParams(vmem_limit_bytes=16 << 20),
        name="attend",
    )(tiles, kv, queries)


def solution(mesh):
    return jax.shard_map(
        shards,
        mesh=mesh,
        in_specs=(
            P(("grp", "fsdp"), "tp"),
            P("tp"),
            P(("tp", "fsdp"), None),
            P("fsdp"),
            P(("grp", "fsdp"), "tp"),
        ),
        out_specs=P(("grp", "fsdp"), "tp"),
        check_vma=False,
    )
```

```python
import jax
import jax.numpy as jnp
from jax import lax
from jax.experimental import pallas as pl
from jax.experimental.pallas import tpu as pltpu
from jax.sharding import PartitionSpec as P

D = 8192
HD = 128
KVH = 4
QH = 32
TILE_TOK = 16
SAMP = 2
TXT_S = 128
CAP = 64
IMG = 128
NX = 4
NZ = 16
FAR = 6
PIECE = 32
PART = 512
SPARE = 2
TURN = (2, 1, 3, 0)
MESH = pl.DeviceIdType.MESH


def project(
    rows_hbm, gain_hbm, w_hbm, out_ref,
    rows, gain_ref, inbox, normed, wz, mine, theirs, kept, packed, parts, half, stat, scale, scale_in,
    local_sem, rows_send, rows_recv, stat_send, stat_recv, scale_send, scale_recv,
    far_send, far_recv, near_send, near_recv, core_send, core_recv, half_send, half_recv, part_send, part_recv, ready,
):
    g = lax.axis_index("grp")
    f = lax.axis_index("fsdp")
    t = lax.axis_index("tp")
    x, z = f // NZ, f % NZ
    ylo, core = t // 2, t % 2

    def xs(step):
        return (x + step + NX) % NX

    def zs(step):
        return (z + step + NZ) % NZ

    def chip(gg, x1, z1, t1):
        return (gg, x1 * NZ + z1, t1)

    barrier = pltpu.get_barrier_semaphore()

    def hello(dev):
        pl.semaphore_signal(barrier, inc=1, device_id=dev, device_id_type=MESH)

    def copy(src, dst, ssem, rsem, dev):
        return pltpu.make_async_remote_copy(
            src_ref=src, dst_ref=dst, send_sem=ssem, recv_sem=rsem, device_id=dev, device_id_type=MESH
        )

    def got(dst, rsem):
        pltpu.make_async_copy(dst, dst, rsem).wait()

    def way(d):
        return 1 if d == 0 else -1

    @pl.when(g == SPARE)
    def _():
        pl.semaphore_wait(barrier, 4)

    @pl.when(g != SPARE)
    def _():
        own_w = pltpu.make_async_copy(w_hbm, wz.at[z], local_sem.at[0])
        own_gain = pltpu.make_async_copy(gain_hbm, gain_ref, local_sem.at[1])
        own_rows = pltpu.make_async_copy(rows_hbm, rows, local_sem.at[2])
        own_w.start()
        own_gain.start()
        for d in (1, -1, FAR, -FAR):
            hello(chip(g, x, zs(d), t))

        @pl.when(g == 0)
        def _():
            own_rows.start()
            for d in (1, 2, 3):
                hello((0, f, (t + d) % 4))
                hello(chip(0, xs(d), z, t))
            for gg in (1, 3):
                for xd in range(NX):
                    hello(chip(gg, xs(xd), z, t))
            for xd in range(NX):
                hello(chip(SPARE, xs(xd), z, (1 - ylo) * 2 + core))

        @pl.when(g > 0)
        def _():
            for xd in range(NX):
                hello(chip(0, xs(xd), z, t))
                hello(chip(g, xs(xd), z, (1 - ylo) * 2 + core))
            for xd in (1, 2, 3):
                hello(chip(g, xs(xd), z, t))
            hello((g, f, ylo * 2 + 1 - core))

        own_w.wait()
        own_gain.wait()

        @pl.when(g == 0)
        def _():
            pl.semaphore_wait(barrier, 18)

        @pl.when(g > 0)
        def _():
            pl.semaphore_wait(barrier, 16)

        sends = []

        def push(*a):
            c = copy(*a)
            c.start()
            sends.append(c)

        def cols(c):
            return pl.ds(c * PART, PART)

        def moved(o, d):
            return o - way(d)

        def cut(o, d):
            return pl.ds(16 * d, 16) if abs(o) == NZ // 2 else pl.ds(0, PIECE)

        def near(o, d, c):
            m = moved(o, d)
            ref = wz.at[zs(o), cut(m, d), cols(c)]
            push(ref, ref, near_send.at[d, c, m % NZ], near_recv.at[d, c, m % NZ], chip(g, x, zs(way(d)), t))

        def got_near(o, d, c):
            got(wz.at[zs(o), cut(o, d), cols(c)], near_recv.at[d, c, o % NZ])

        for c in (0, 1):
            for d in (0, 1):
                ref = wz.at[z, :, cols(c)]
                push(ref, ref, far_send.at[d, c], far_recv.at[d, c], chip(g, x, zs(FAR * way(d)), t))

        def rows_copy(i, gg, block, xd):
            src = rows_hbm.at[pl.ds(block * IMG, IMG), pl.ds(pl.multiple_of(xs(xd) * PART, PART), PART)]
            return copy(src, inbox.at[x], rows_send.at[i, xd], rows_recv.at[x], chip(gg, xs(xd), z, t))

        targets = ((1, 0), (3, 2), (0, 1))

        def own_inbox():
            src = rows_hbm.at[pl.ds(IMG, IMG), pl.ds(pl.multiple_of(x * PART, PART), PART)]
            return pltpu.make_async_copy(src, inbox.at[x], rows_recv.at[x])

        @pl.when(g == 0)
        def _():
            own_inbox().start()
            for xd in TURN[:3]:
                rows_copy(2, 0, 1, xd).start()
            for xd in TURN:
                for i, (gg, block) in enumerate(targets[:2]):
                    rows_copy(i, gg, block, xd).start()

        for c in (0, 1):
            for d in (0, 1):
                near(0, d, c)

        def stat_copy(d):
            return copy(stat.at[0], stat.at[d], stat_send.at[d - 1], stat_recv.at[d - 1], (0, f, (t + d) % 4))

        for c in (0, 1):
            for d in (0, 1):
                got_near(-way(d), d, c)
                near(-way(d), d, c)

        def scale_copy(i, gg, block, xd):
            return copy(
                scale.at[block], scale_in.at[x], scale_send.at[i, xd], scale_recv.at[x], chip(gg, xs(xd), z, t)
            )

        for c in (0, 1):
            for d in (0, 1):
                got(wz.at[zs(-FAR * way(d)), :, cols(c)], far_recv.at[d, c])
            for d in (0, 1):
                near(-FAR * way(d), d, c)
                near(FAR * way(d), d, c)
        @pl.when(g == 0)
        def _():
            own_rows.wait()
            total = jnp.zeros((3 * IMG, 128), jnp.float32)
            for j in range(NZ):
                part = rows[:, j * 128:(j + 1) * 128].astype(jnp.float32)
                total = total + part * part
            line = jnp.sum(jnp.transpose(total), axis=0, keepdims=True)
            stat[0] = jnp.broadcast_to(line, (8, 3 * IMG))
            for d in (1, 2, 3):
                stat_copy(d).start()

        for c in (0, 1):
            for d in (0, 1):
                got_near(-2 * way(d), d, c)
                near(-2 * way(d), d, c)
        @pl.when(g == 0)
        def _():
            for d in (1, 2, 3):
                got(stat.at[d], stat_recv.at[d - 1])
            both = (stat[0] + stat[1]) + (stat[2] + stat[3])
            inv = lax.rsqrt(both / D + 1e-05)
            for block in range(3):
                scale[block] = inv[:, block * IMG:(block + 1) * IMG]
            for xd in range(NX):
                for i, (gg, block) in enumerate(targets):
                    if gg == 0 and xd == 0:
                        pltpu.make_async_copy(scale.at[block], scale_in.at[x], scale_recv.at[x]).start()
                    else:
                        scale_copy(i, gg, block, xd).start()

        for c in (0, 1):
            for d in (0, 1):
                got_near(-7 * way(d), d, c)
                near(-7 * way(d), d, c)
                got_near(5 * way(d), d, c)
                near(5 * way(d), d, c)

        gains = []
        for j in range(PART // 128):
            pick = gain_ref[j * 128:(j + 1) * 128]
            for i in (1, 2, 3):
                pick = jnp.where(x == i, gain_ref[i * PART + j * 128:i * PART + (j + 1) * 128], pick)
            gains.append(pick.astype(jnp.float32).reshape(1, 128))
        for c in (0, 1):
            for d in (0, 1):
                got_near(-3 * way(d), d, c)
                got_near(-8 * way(d), d, c)
                got_near(4 * way(d), d, c)

        slot = x * 2 + ylo

        def side(j):
            return ylo if j == 0 else 1 - ylo

        def head(i, h):
            w = wz[:, :, pl.ds(pl.multiple_of(h * 256, 256), 256)].reshape(PART, 256)
            return jnp.dot(normed[i], w, preferred_element_type=jnp.float32)

        partner = (0, f, (1 - ylo) * 2 + core)

        def across(i):
            return copy(packed.at[i, 0], half.at[i], half_send.at[i], half_recv.at[i], partner)

        def part_copy(i, j, xd):
            gg = SPARE if j == 2 else g
            return copy(
                packed.at[i, min(j, 1)], parts.at[slot], part_send.at[min(j, 1), xd], part_recv.at[slot],
                chip(gg, xs(-xd), z, side(min(j, 1)) * 2 + core),
            )

        def begin(i, xd):
            src = xs(-xd)
            got(inbox.at[src], rows_recv.at[src])
            if i == 0:
                for k in range(NX):
                    got(scale_in.at[k], scale_recv.at[k])
            column = jnp.transpose(jnp.broadcast_to(scale_in[src, 0:1], (128, IMG)))
            for j in range(PART // 128):
                lanes = slice(j * 128, (j + 1) * 128)
                normed[i, :, lanes] = (
                    inbox[src, :, lanes].astype(jnp.float32) * column * gains[j]
                ).astype(jnp.bfloat16)
            for j in (0, 1):
                mine[i, j] = head(i, side(j) * 2 + 1 - core)
            push(mine.at[i], theirs.at[i], core_send.at[i], core_recv.at[i], (g, f, ylo * 2 + 1 - core))
            for j in (0, 1):
                kept[i, j] = head(i, side(j) * 2 + core)

        def finish(i, xd):
            got(theirs.at[i], core_recv.at[i])

            @pl.when(g == 0)
            def _():
                packed[i, 0] = (kept[i, 0] + theirs[i, 0]).astype(jnp.bfloat16)
                across(i).start()

            @pl.when(g > 0)
            def _():
                for j in (1, 0):
                    packed[i, j] = (kept[i, j] + theirs[i, j]).astype(jnp.bfloat16)
                    if j == 0 and xd == 0:
                        pltpu.make_async_copy(packed.at[i, j], parts.at[slot], part_recv.at[slot]).start()
                    else:
                        part_copy(i, j, xd).start()

        def final(i, xd):
            @pl.when(g == 0)
            def _():
                if i == 0:
                    pl.semaphore_wait(ready, 4)
                got(half.at[i], half_recv.at[i])
                packed[i, 1] = (
                    (kept[i, 1] + theirs[i, 1]) + half[i].astype(jnp.float32)
                ).astype(jnp.bfloat16)
                part_copy(i, 2, xd).start()

        for i in range(NX):
            begin(i, TURN[i])
            if i >= 1:
                finish(i - 1, TURN[i - 1])
            if i >= 2:
                final(i - 2, TURN[i - 2])
        finish(NX - 1, TURN[NX - 1])
        final(NX - 2, TURN[NX - 2])
        final(NX - 1, TURN[NX - 1])

        @pl.when(g > 0)
        def _():
            for i, xd in enumerate(TURN):
                for j in (1, 0):
                    if j == 1 or xd != 0:
                        part_copy(i, j, xd).wait_send()

        @pl.when(g == 0)
        def _():
            for i, xd in enumerate(TURN):
                across(i).wait_send()
                part_copy(i, 2, xd).wait_send()
            for d in (1, 2, 3):
                stat_copy(d).wait_send()
            for xd in range(NX):
                for i, (gg, block) in enumerate(targets):
                    if gg != 0 or xd != 0:
                        rows_copy(i, gg, block, xd).wait_send()
                        scale_copy(i, gg, block, xd).wait_send()

        for c in sends:
            c.wait_send()

    @pl.when(g == SPARE)
    def _():
        for xd in range(NX):
            pl.semaphore_signal(
                ready, inc=1, device_id=chip(0, xs(xd), z, (1 - ylo) * 2 + core), device_id_type=MESH
            )

    def gather_parts(slots):
        total = jnp.zeros((IMG, 2 * HD), jnp.float32)
        for i in slots:
            got(parts.at[i], part_recv.at[i])
            total = total + parts[i].astype(jnp.float32)
        out_ref[...] = total.astype(jnp.bfloat16)

    @pl.when(g == SPARE)
    def _():
        gather_parts([xs(-xd) * 2 + 1 - ylo for xd in TURN])

    @pl.when((g > 0) & (g != SPARE))
    def _():
        gather_parts(range(2 * NX))


def attend(tiles_ref, kv_ref, q_ref, o_ref):
    g = lax.axis_index("grp")

    @pl.when(g == 0)
    def _():
        o_ref[...] = jnp.zeros_like(o_ref)

    @pl.when(g > 0)
    def _():
        slot = lax.broadcasted_iota(jnp.int32, (TXT_S, CAP), 1)
        for s in range(SAMP):
            keys = kv_ref[s * CAP:(s + 1) * CAP, :HD]
            values = kv_ref[s * CAP:(s + 1) * CAP, HD:]
            live = slot < tiles_ref[(g - 1) * SAMP + s] * TILE_TOK
            for h in range(QH // KVH):
                q = q_ref[s * TXT_S:(s + 1) * TXT_S, h * HD:(h + 1) * HD]
                scores = lax.dot_general(
                    q, keys, (((1,), (1,)), ((), ())), preferred_element_type=jnp.float32
                ) * (1.0 / HD**0.5)
                scores = jnp.where(live, scores, -1e30)
                expo = jnp.exp(scores - jnp.max(scores, axis=-1, keepdims=True))
                weights = (expo / jnp.sum(expo, axis=-1, keepdims=True)).astype(jnp.bfloat16)
                o_ref[s * TXT_S:(s + 1) * TXT_S, h * HD:(h + 1) * HD] = jnp.dot(
                    weights, values, preferred_element_type=jnp.float32
                ).astype(jnp.bfloat16)


def shards(image_rows, enc_gain, key_value_w, tiles, queries):
    dma = pltpu.SemaphoreType.DMA
    bf16, f32 = jnp.bfloat16, jnp.float32
    hbm = pl.BlockSpec(memory_space=pltpu.HBM)
    vmem = pl.BlockSpec(memory_space=pltpu.VMEM)
    kv = pl.pallas_call(
        project,
        out_shape=jax.ShapeDtypeStruct((IMG, 2 * HD), bf16),
        in_specs=[hbm, hbm, hbm],
        out_specs=vmem,
        scratch_shapes=[
            pltpu.VMEM((3 * IMG, 2048), bf16),
            pltpu.VMEM((2048,), bf16),
            pltpu.VMEM((NX, IMG, PART), bf16),
            pltpu.VMEM((NX, IMG, PART), bf16),
            pltpu.VMEM((NZ, PIECE, 1024), bf16),
            pltpu.VMEM((NX, 2, IMG, 256), f32),
            pltpu.VMEM((NX, 2, IMG, 256), f32),
            pltpu.VMEM((NX, 2, IMG, 256), f32),
            pltpu.VMEM((NX, 2, IMG, 256), bf16),
            pltpu.VMEM((2 * NX, IMG, 256), bf16),
            pltpu.VMEM((NX, IMG, 256), bf16),
            pltpu.VMEM((4, 8, 3 * IMG), f32),
            pltpu.VMEM((3, 8, IMG), f32),
            pltpu.VMEM((NX, 8, IMG), f32),
            dma((3,)),
            dma((3, NX)),
            dma((NX,)),
            dma((3,)),
            dma((3,)),
            dma((3, NX)),
            dma((NX,)),
            dma((2, 2)),
            dma((2, 2)),
            dma((2, 2, NZ)),
            dma((2, 2, NZ)),
            dma((NX,)),
            dma((NX,)),
            dma((NX,)),
            dma((NX,)),
            dma((2, NX)),
            dma((2 * NX,)),
            pltpu.SemaphoreType.REGULAR,
        ],
        compiler_params=pltpu.CompilerParams(
            collective_id=0, has_side_effects=True, vmem_limit_bytes=63 << 20
        ),
        name="project",
    )(image_rows, enc_gain, key_value_w)
    return pl.pallas_call(
        attend,
        out_shape=jax.ShapeDtypeStruct(queries.shape, bf16),
        in_specs=[pl.BlockSpec(memory_space=pltpu.SMEM), vmem, vmem],
        out_specs=vmem,
        compiler_params=pltpu.CompilerParams(vmem_limit_bytes=16 << 20),
        name="attend",
    )(tiles, kv, queries)


def solution(mesh):
    return jax.shard_map(
        shards,
        mesh=mesh,
        in_specs=(
            P(("grp", "fsdp"), "tp"),
            P("tp"),
            P(("tp", "fsdp"), None),
            P("fsdp"),
            P(("grp", "fsdp"), "tp"),
        ),
        out_specs=P(("grp", "fsdp"), "tp"),
        check_vma=False,
    )
```
